32 devices in a mesh: gx: 4 (over y, x), gy: 2 (over core), gz: 4 (over z).
Axes of the slice: x: 2, y: 2, z: 4, core: 2. Of those that a mesh axis runs over, the one named last changes fastest.
Arguments:
- fields: float32 [64, 8, 16, 256], P(('gx', 'gy', 'gz')), may hold values from 0 to 1
- seed_labels: int32 [64, 256], P(('gx', 'gy', 'gz')), may hold values from 0 to 3
- coords: int32 [48, 3], replicated, may hold values from 0 to 5, as said below
- neighbours: int32 [48, 6], replicated, may hold values from -1 to 47, as said below
- owner_before: int32 [48], replicated, may hold values from 0 to 63, as said below
- owner_after: int32 [48], replicated, may hold values from 0 to 63, as said below
- couple: float32 [4, 4], replicated, may hold values from -3 to 3
- latent: float32 [4, 4], replicated, may hold values from -3 to 3
- diffuse: float32 [4], replicated, may hold values from 0.3 to 1.5
- thermal_gain: float32 [4], replicated, may hold values from -4 to 4
Outputs:
- fields_out: float32 [64, 8, 16, 256], P(('gx', 'gy', 'gz'))
The draws below stay inside these ranges and needn't reach their ends.
Inputs may be any that keep to these rules, and one draw needn't show every extreme that they name: `coords`: a permutation of the positions of a 4 x 2 x 6 grid of blocks. `neighbours`: the block beside b across each side by coords; -1 beyond the ends along x and y; along z the blocks close into a loop. `owner_before`: distinct for distinct blocks; a place p is slot p % 2 of device p // 2, devices counted over gx, gy, gz in order; block b's device has index coords[b, 0] along gx and coords[b, 1] along gy. `owner_after`: distinct for distinct blocks; a block's device after migration is its device before or the next one along gz, cyclic, with the same gx and gy indices; at most one block of a device moves; in every group of devices along gz at least one block moves.
All inputs are finite; a program needn't handle non-finite values.
Results may differ from the reference program's by a relative error of at most 0.0003.
Values sent between devices are 32-bit elements; how exact they have to be, the bound alone decides.
A program may use at most 64 MiB of HBM per device.

```python
import math
import jax
import jax.numpy as jnp
from jax import lax

CB = 16
NPHASE = 4
NPOT = 4
STEPS = 2
BLX = 4
BLY = 2
BLZ = 6
NBLK = 48
SLOTS_ALL = 64


def layout(key):
    base = jax.random.fold_in(key, 101)
    streams = jax.random.split(base, 6)
    cycle_len = BLZ * 2 // 3
    columns = BLX * BLY
    spare_slots = 2 * (cycle_len - 2)
    rotation = jax.random.randint(streams[0], (columns,), 0, cycle_len)
    picks = jax.vmap(lambda sub_key: jax.random.permutation(sub_key, spare_slots))(jax.random.split(streams[1], columns))
    picks = picks[:, :BLZ - 2].astype(jnp.int32)
    relative = jnp.concatenate([jnp.zeros((columns, 2), jnp.int32), picks // 2 + 2], 1)
    slot_pick = jnp.concatenate([jnp.tile(jnp.array([[0, 1]], jnp.int32), (columns, 1)), picks % 2], 1)
    depth_of = jax.vmap(lambda sub_key: jax.random.permutation(sub_key, BLZ))(jax.random.split(streams[2], columns)).astype(jnp.int32)
    loads = jnp.sum((relative[:, :, None] == jnp.arange(cycle_len, dtype=jnp.int32)[None, None, :]).astype(jnp.int32), 1)
    mover = jnp.logical_and(loads == 2, jnp.roll(loads, -1, axis=1) == 0)
    leave_bit = jax.random.randint(streams[3], (columns, cycle_len), 0, 2)
    land_bit = jax.random.randint(streams[4], (columns, cycle_len), 0, 2)
    moving = jnp.logical_and(jnp.take_along_axis(mover, relative, 1), slot_pick == jnp.take_along_axis(leave_bit, relative, 1))
    after_rel = relative + moving.astype(jnp.int32)
    after_slot = jnp.where(moving, jnp.take_along_axis(land_bit, relative, 1), slot_pick).astype(jnp.int32)
    column_ids = jnp.arange(columns, dtype=jnp.int32)[:, None]
    cycle_before = (rotation[:, None] + relative) % cycle_len
    cycle_after = (rotation[:, None] + after_rel) % cycle_len
    own_before = (column_ids * cycle_len + cycle_before) * 2 + slot_pick
    own_after = (column_ids * cycle_len + cycle_after) * 2 + after_slot
    ident = jax.random.permutation(streams[5], NBLK).astype(jnp.int32)
    position = column_ids * BLZ + depth_of
    block_of_entry = ident[position].reshape(-1)
    owners_first = jnp.zeros((NBLK,), jnp.int32).at[block_of_entry].set(own_before.reshape(-1).astype(jnp.int32))
    owners_second = jnp.zeros((NBLK,), jnp.int32).at[block_of_entry].set(own_after.reshape(-1).astype(jnp.int32))
    places = jnp.arange(NBLK, dtype=jnp.int32)
    grid_x = places // (BLY * BLZ)
    grid_y = places // BLZ % BLY
    grid_z = places % BLZ
    coords_pos = jnp.stack([grid_x, grid_y, grid_z], 1)
    coords_all = jnp.zeros((NBLK, 3), jnp.int32).at[ident].set(coords_pos)
    beside = jnp.stack([jnp.where(grid_x > 0, places - BLY * BLZ, -1), jnp.where(grid_x < BLX - 1, places + BLY * BLZ, -1), jnp.where(grid_y > 0, places - BLZ, -1), jnp.where(grid_y < BLY - 1, places + BLZ, -1), places - grid_z + (grid_z + BLZ - 1) % BLZ, places - grid_z + (grid_z + 1) % BLZ], 1)
    beside_ids = jnp.where(beside >= 0, ident[jnp.maximum(beside, 0)], -1).astype(jnp.int32)
    neighbour_all = jnp.zeros((NBLK, 6), jnp.int32).at[ident].set(beside_ids)
    return (coords_all, neighbour_all, owners_first, owners_second)


def draw_coords(key, part):
    return layout(key)[0]


def draw_neighbours(key, part):
    return layout(key)[1]


def draw_owner_before(key, part):
    return layout(key)[2]


def draw_owner_after(key, part):
    return layout(key)[3]


def set_ends(values, stream_key, smallest, top_value):
    longest = values.shape.index(max(values.shape))
    spots = []
    for shift in (0, 1):
        where = [jax.random.randint(jax.random.fold_in(stream_key, axis), (), 0, length) for axis, length in enumerate(values.shape)]
        where[longest] = (where[longest] + shift) % values.shape[longest]
        spots.append(tuple(where))
    return values.at[spots[0]].set(smallest).at[spots[1]].set(top_value)


def block_scale(key, dims, cuts, smallest, high):
    def one(dim, blocks):
        draws = jax.random.uniform(jax.random.fold_in(jax.random.fold_in(key, 6), dim), (blocks,), jnp.float32, smallest / len(cuts), high / len(cuts))
        return jnp.repeat(jnp.exp(draws), dims[dim] // blocks).reshape((-1,) + (1,) * (len(dims) - dim - 1))

    loudness = one(*cuts[0])
    for cut in cuts[1:]:
        loudness = loudness * one(*cut)
    return loudness


def centred(key, shape, scale, reach, kind=jnp.bfloat16):
    return jnp.clip(scale * jax.random.normal(key, shape, jnp.float32), -reach, reach).astype(kind)


def setup_inputs(seed: int = 0) -> dict:
    key_list = jax.random.split(jax.random.key(seed), 11)
    return {
        "fields": jnp.clip(1.0 * jax.random.uniform(key_list[0], (SLOTS_ALL, NPHASE + NPOT, CB, CB * CB), jnp.float32) ** block_scale(key_list[0], (SLOTS_ALL, NPHASE + NPOT, CB, CB * CB), ((0, 32),), -0.2, 0.2), 0.0, 1.0),
        "seed_labels": set_ends(jax.random.randint(key_list[1], (SLOTS_ALL, CB * CB), 0, NPHASE), jax.random.fold_in(key_list[1], 1), 0, NPHASE - 1).astype(jnp.int32),
        "coords": draw_coords(jax.random.fold_in(key_list[10], 71), 0),
        "neighbours": draw_neighbours(jax.random.fold_in(key_list[10], 71), 0),
        "owner_before": draw_owner_before(jax.random.fold_in(key_list[10], 71), 0),
        "owner_after": draw_owner_after(jax.random.fold_in(key_list[10], 71), 0),
        "couple": centred(key_list[6], (NPHASE, NPOT), NPOT ** -0.5, 3.0, jnp.float32),
        "latent": centred(key_list[7], (NPOT, NPHASE), 0.5, 3.0, jnp.float32),
        "diffuse": jnp.clip(jnp.exp(jax.random.uniform(key_list[8], (NPOT,), jnp.float32, math.log(0.3), math.log(1.5))), 0.3, 1.5),
        "thermal_gain": centred(key_list[9], (NPHASE,), 1.0, 4.0, jnp.float32),
    }


OPPOSITE = (1, 0, 3, 2, 5, 4)
seed_gain = 2.0


def faces_of(volume):
    components, extent, surface = volume.shape
    low_x = volume[:, 0, :]
    high_x = volume[:, extent - 1, :]
    low_y = volume[:, :, :extent].reshape(components, extent * extent)
    high_y = volume[:, :, surface - extent:].reshape(components, extent * extent)
    low_z = volume[:, :, 0::extent].reshape(components, extent * extent)
    high_z = volume[:, :, extent - 1::extent].reshape(components, extent * extent)
    return jnp.stack([low_x, high_x, low_y, high_y, low_z, high_z], 0)


def laplace(volume, ghosts):
    components, extent, surface = volume.shape
    below_x = jnp.concatenate([ghosts[0][:, None, :], volume[:, :-1, :]], 1)
    above_x = jnp.concatenate([volume[:, 1:, :], ghosts[1][:, None, :]], 1)
    below_y = jnp.concatenate([ghosts[2].reshape(components, extent, extent), volume[:, :, :-extent]], 2)
    above_y = jnp.concatenate([volume[:, :, extent:], ghosts[3].reshape(components, extent, extent)], 2)
    offset_z = jnp.arange(surface) % extent
    zeros_col = jnp.zeros((components, extent, 1), volume.dtype)
    below_z = jnp.where(offset_z == 0, jnp.repeat(ghosts[4].reshape(components, extent, extent), extent, axis=2),
                        jnp.concatenate([zeros_col, volume[:, :, :-1]], 2))
    above_z = jnp.where(offset_z == extent - 1, jnp.repeat(ghosts[5].reshape(components, extent, extent), extent, axis=2),
                        jnp.concatenate([volume[:, :, 1:], zeros_col], 2))
    return below_x + above_x + below_y + above_y + below_z + above_z - 6.0 * volume


def phase_step(phases, potential, ghosts, x_global, seed_row, iteration, couple, thermal_gain, seeded):
    extent = phases.shape[1]
    thermal = x_global / (2.0 * extent) - 1.0 - 0.25 * iteration
    driving = jnp.einsum('kj,jxc->kxc', couple, potential, precision=lax.Precision.HIGHEST)
    driving = driving + thermal_gain[:, None, None] * thermal[None, :, None]
    if seeded:
        marks = seed_row[None, None, :] == jnp.arange(phases.shape[0], dtype=jnp.int32)[:, None, None]
        driving = driving + seed_gain * marks.astype(jnp.float32)
    return phases + 0.12 * laplace(phases, ghosts) + phases * (1.0 - phases) * (phases - 0.5 + driving)


def potential_step(potential, ghosts, old_phases, new_phases, diffuse, latent):
    release = jnp.einsum('jk,kxc->jxc', latent, new_phases - old_phases, precision=lax.Precision.HIGHEST)
    return potential + 0.1 * diffuse[:, None, None] * laplace(potential, ghosts) - release


def ghosts_of(values, neighbours):
    surfaces = jax.vmap(faces_of)(values)
    present = neighbours >= 0
    safe_ids = jnp.where(present, neighbours, 0)
    picked = jnp.stack([surfaces[safe_ids[:, side], OPPOSITE[side]] for side in range(6)], 1)
    return jnp.where(present[:, :, None, None], picked, surfaces)


def reference(fields, seed_labels, coords, neighbours, owner_before, owner_after, couple, latent, diffuse, thermal_gain):
    blocks = fields[owner_before]
    seed_rows = seed_labels[owner_before]
    x_global = (coords[:, 0:1] * CB + jnp.arange(CB, dtype=jnp.int32)[None, :]).astype(jnp.float32)
    phases = blocks[:, :NPHASE]
    potential = blocks[:, NPHASE:]
    for iteration in range(STEPS):
        phase_ghost = ghosts_of(phases, neighbours)
        new_phases = lax.map(
            lambda member: phase_step(member[0], member[1], member[2], member[3], member[4],
                                      iteration, couple, thermal_gain, iteration == 0),
            (phases, potential, phase_ghost, x_global, seed_rows))
        pot_ghost = ghosts_of(potential, neighbours)
        potential = lax.map(
            lambda member: potential_step(member[0], member[1], member[2], member[3], diffuse, latent),
            (potential, pot_ghost, phases, new_phases))
        phases = new_phases
    result = jnp.concatenate([phases, potential], 1)
    return jnp.zeros_like(fields).at[owner_after].set(result)
```

```python
import functools

import jax
import jax.numpy as jnp
from jax import lax
from jax.experimental import pallas as pl
from jax.experimental.pallas import tpu as pltpu
from jax.sharding import PartitionSpec as P

NPHASE = 4
STEPS = 2
LANES = 128
SEED_GAIN = 2.0
MESH = pl.DeviceIdType.MESH


def kernel(
    sizes,
    fields,
    seeds,
    coords,
    before,
    after,
    couple,
    latent,
    diffuse,
    gain,
    out,
    recv,
    seed_recv,
    vals,
    xsend,
    xghost,
    ysend,
    yghost,
    result,
    outbuf,
    in_send,
    in_recv,
    seed_send,
    seed_got,
    x_send,
    x_recv,
    y_send,
    y_recv,
    out_send,
    out_recv,
    local_sem,
):
    gx_n, gy_n, gz_n, nblk, cells, surface = sizes
    slots, nfield = outbuf.shape[1], outbuf.shape[2]
    rows = outbuf.shape[3]
    halves = surface // LANES
    per_column = vals.shape[1]
    x_parts = gz_n // halves
    gx, gy, gz = lax.axis_index("gx"), lax.axis_index("gy"), lax.axis_index("gz")
    odd_x, odd_y = gx % 2, gy % 2

    def part_of(g):
        a, b = g // halves, g % halves
        xh = a + odd_x * (x_parts - 1 - 2 * a)
        yh = b + odd_y * (halves - 1 - 2 * b)
        return xh, yh

    def window(ref, g):
        xh, yh = part_of(g)
        x0 = pl.multiple_of(xh * rows, rows)
        y0 = pl.multiple_of(yh * LANES, LANES)
        return ref.at[:, :, pl.ds(x0, rows), pl.ds(y0, LANES)]

    def seed_window(g):
        _, yh = part_of(g)
        return seeds.at[:, pl.ds(pl.multiple_of(yh * LANES, LANES), LANES)]

    xh, yh = part_of(gz)
    xpos = gx * x_parts + xh
    ypos = gy * halves + yh
    x_total, y_total = gx_n * x_parts, gy_n * halves
    dir_x = 1 - 2 * odd_x
    dir_y = 1 - 2 * odd_y
    xlo_in, xhi_in = xh > 0, xh < x_parts - 1
    ylo_in, yhi_in = yh > 0, yh < halves - 1
    sides = []
    for exists, inside, step_x, step_y, move in (
        (xpos > 0, xlo_in, -1, 0, -halves * dir_x),
        (xpos < x_total - 1, xhi_in, 1, 0, halves * dir_x),
        (ypos > 0, ylo_in, 0, -1, -dir_y),
        (ypos < y_total - 1, yhi_in, 0, 1, dir_y),
    ):
        ins = inside.astype(jnp.int32)
        device = (gx + step_x * (1 - ins), gy + step_y * (1 - ins), gz + move * ins)
        sides.append((exists, inside, device))

    barrier = pltpu.get_barrier_semaphore()
    for d in range(1, gz_n):
        pl.semaphore_signal(
            barrier, inc=1, device_id=(gx, gy, (gz + d) % gz_n), device_id_type=MESH
        )
    expected = gz_n - 1
    for exists, inside, device in sides:
        outside = jnp.logical_and(exists, jnp.logical_not(inside))

        @pl.when(outside)
        def _(device=device):
            pl.semaphore_signal(barrier, inc=1, device_id=device, device_id_type=MESH)

        expected = expected + outside.astype(jnp.int32)
    pl.semaphore_wait(barrier, expected)

    moves = []
    for d in range(gz_n - 1, 0, -1):
        to = (gz + d) % gz_n
        for src, dst, s_sem, r_sem in (
            (window(fields, to), recv.at[pl.ds(slots * gz, slots)], in_send, in_recv),
            (seed_window(to), seed_recv.at[gz], seed_send, seed_got),
        ):
            copy = pltpu.make_async_remote_copy(
                src_ref=src,
                dst_ref=dst,
                send_sem=s_sem.at[d - 1],
                recv_sem=r_sem.at[d - 1],
                device_id=(gx, gy, to),
                device_id_type=MESH,
            )
            copy.start()
            moves.append(copy)
    own = pltpu.make_async_copy(
        window(fields, gz), recv.at[pl.ds(slots * gz, slots)], local_sem.at[0]
    )
    own.start()
    own_seed = pltpu.make_async_copy(seed_window(gz), seed_recv.at[gz], local_sem.at[1])
    own_seed.start()

    base = (gx * gy_n + gy) * (gz_n * slots)
    places = gz_n * slots

    def lookup(b, carry):
        source, depth = carry
        here = jnp.logical_and(coords[0, b] == gx, coords[1, b] == gy)
        z = jnp.where(here, coords[2, b], -1)
        was = before[b] - base
        now = jnp.where(here, after[b] - base, -1)
        source = tuple(jnp.where(z == k, was, source[k]) for k in range(per_column))
        depth = tuple(jnp.where(now == q, z, depth[q]) for q in range(places))
        return source, depth

    source, depth = lax.fori_loop(
        0,
        nblk,
        lookup,
        ((jnp.int32(0),) * per_column, (jnp.int32(-1),) * places),
    )

    own.wait()
    own_seed.wait()
    for copy in moves:
        copy.wait()

    marks = []
    for k in range(per_column):
        p = source[k]
        vals[:, k] = recv[p]
        pair = seed_recv[p // slots]
        row = pair[0:1]
        for s in range(1, slots):
            row = jnp.where(p % slots == s, pair[s : s + 1], row)
        marks.append(row[None])
    marks = jnp.concatenate(marks, 0)

    shape = (per_column, rows, LANES)
    lane = lax.broadcasted_iota(jnp.int32, shape, 2)
    row_id = lax.broadcasted_iota(jnp.int32, shape, 1)
    z_cell = lane % cells
    group = lane // cells
    xglob = (row_id + (gx * cells + xh * rows)).astype(jnp.float32)

    def rolled(v, shift):
        shift = shift % LANES
        return v if shift == 0 else pltpu.roll(v, shift, 2)

    def exchange(step, old):
        low_y = jnp.zeros(shape, jnp.float32)
        high_y = low_y
        for f in range(nfield):
            v = old[f]
            xsend[step, 0, :, f : f + 1, :] = v[:, 0:1, :]
            xsend[step, 1, :, f : f + 1, :] = v[:, rows - 1 : rows, :]
            low_y = jnp.where(group == f, rolled(v, cells * f), low_y)
            high_y = jnp.where(group == f, rolled(v, cells * f + cells), high_y)
        ysend[step, 0] = low_y
        ysend[step, 1] = high_y
        for phase in ("start", "wait"):
            for side, (exists, _, device) in enumerate(sides):
                send, ghost, s_sem, r_sem = (
                    (xsend, xghost, x_send, x_recv)
                    if side < 2
                    else (ysend, yghost, y_send, y_recv)
                )
                e = side % 2

                @pl.when(exists)
                def _(send=send, ghost=ghost, s_sem=s_sem, r_sem=r_sem, e=e, device=device):
                    if phase == "start":
                        pltpu.make_async_remote_copy(
                            src_ref=send.at[step, e],
                            dst_ref=ghost.at[step, 1 - e],
                            send_sem=s_sem.at[step, e],
                            recv_sem=r_sem.at[step, 1 - e],
                            device_id=device,
                            device_id_type=MESH,
                        ).start()
                    else:
                        pltpu.make_async_remote_copy(
                            src_ref=send.at[step, e],
                            dst_ref=ghost.at[step, e],
                            send_sem=s_sem.at[step, e],
                            recv_sem=r_sem.at[step, e],
                            device_id=device,
                            device_id_type=MESH,
                        ).wait()

                if phase == "start":

                    @pl.when(jnp.logical_not(exists))
                    def _(send=send, ghost=ghost, e=e):
                        ghost[step, e] = send[step, e]

    def laplace(step, f, v):
        below_x = jnp.concatenate([xghost[step, 0, :, f : f + 1, :], v[:, :-1, :]], 1)
        above_x = jnp.concatenate([v[:, 1:, :], xghost[step, 1, :, f : f + 1, :]], 1)
        below_y = jnp.where(
            group == 0, rolled(yghost[step, 0], -cells * f), rolled(v, cells)
        )
        above_y = jnp.where(
            group == LANES // cells - 1,
            rolled(yghost[step, 1], -cells * f - cells),
            rolled(v, -cells),
        )
        before_k = jnp.concatenate([v[-1:], v[:-1]], 0)
        after_k = jnp.concatenate([v[1:], v[:1]], 0)
        below_z = jnp.where(z_cell == 0, rolled(before_k, 1 - cells), rolled(v, 1))
        above_z = jnp.where(z_cell == cells - 1, rolled(after_k, cells - 1), rolled(v, -1))
        return below_x + above_x + below_y + above_y + below_z + above_z - 6.0 * v

    for step in range(STEPS):
        src = vals if step == 0 else result.at[step - 1]
        exchange(step, [src[f] for f in range(nfield)])
        thermal = xglob / (2.0 * cells) - 1.0 - 0.25 * step
        change = []
        for k in range(NPHASE):
            phi = src[k]
            drive = gain[k] * thermal
            for j in range(nfield - NPHASE):
                drive = drive + couple[k, j] * src[NPHASE + j]
            if step == 0:
                drive = drive + SEED_GAIN * (marks == k).astype(jnp.float32)
            delta = 0.12 * laplace(step, k, phi) + phi * (1.0 - phi) * (phi - 0.5 + drive)
            new = phi + delta
            result[step, k] = new
            change.append(new - phi)
        for j in range(nfield - NPHASE):
            mu = src[NPHASE + j]
            new = mu + (0.1 * diffuse[j]) * laplace(step, NPHASE + j, mu)
            for k in range(NPHASE):
                new = new - latent[j, k] * change[k]
            result[step, NPHASE + j] = new

    for q in range(places):
        k = depth[q]
        tile = result[STEPS - 1, :, jnp.maximum(k, 0)]
        outbuf[q // slots, q % slots] = jnp.where(k >= 0, tile, 0.0)
    moves = []
    for d in range(gz_n - 1, 0, -1):
        to = (gz + d) % gz_n
        copy = pltpu.make_async_remote_copy(
            src_ref=outbuf.at[to],
            dst_ref=window(out, gz),
            send_sem=out_send.at[d - 1],
            recv_sem=out_recv.at[d - 1],
            device_id=(gx, gy, to),
            device_id_type=MESH,
        )
        copy.start()
        moves.append(copy)
    own = pltpu.make_async_copy(outbuf.at[gz], window(out, gz), local_sem.at[2])
    own.start()
    own.wait()
    for copy in moves:
        copy.wait()


def solution(mesh):
    gx_n, gy_n, gz_n = mesh.shape["gx"], mesh.shape["gy"], mesh.shape["gz"]

    def per_device(fields, seeds, coords, neighbours, before, after, couple, latent, diffuse, gain):
        slots, nfield, cells, surface = fields.shape
        nblk = coords.shape[0]
        per_column = nblk // (gx_n * gy_n)
        halves = surface // LANES
        rows = cells * halves // gz_n
        f32, i32 = jnp.float32, jnp.int32
        dma = pltpu.SemaphoreType.DMA
        smem = pl.BlockSpec(memory_space=pltpu.SMEM)
        anyspace = pl.BlockSpec(memory_space=pl.ANY)
        faces_x = (STEPS, 2, per_column, nfield, LANES)
        faces_y = (STEPS, 2, per_column, rows, LANES)
        return pl.pallas_call(
            functools.partial(kernel, (gx_n, gy_n, gz_n, nblk, cells, surface)),
            out_shape=jax.ShapeDtypeStruct(fields.shape, f32),
            in_specs=[anyspace, anyspace] + [smem] * 7,
            out_specs=anyspace,
            scratch_shapes=[
                pltpu.VMEM((gz_n * slots, nfield, rows, LANES), f32),
                pltpu.VMEM((gz_n, slots, LANES), i32),
                pltpu.VMEM((nfield, per_column, rows, LANES), f32),
                pltpu.VMEM(faces_x, f32),
                pltpu.VMEM(faces_x, f32),
                pltpu.VMEM(faces_y, f32),
                pltpu.VMEM(faces_y, f32),
                pltpu.VMEM((STEPS, nfield, per_column, rows, LANES), f32),
                pltpu.VMEM((gz_n, slots, nfield, rows, LANES), f32),
                dma((gz_n,)),
                dma((gz_n,)),
                dma((gz_n,)),
                dma((gz_n,)),
                dma((STEPS, 2)),
                dma((STEPS, 2)),
                dma((STEPS, 2)),
                dma((STEPS, 2)),
                dma((gz_n,)),
                dma((gz_n,)),
                dma((3,)),
            ],
            compiler_params=pltpu.CompilerParams(collective_id=0, has_side_effects=True),
        )(fields, seeds, coords.T, before, after, couple, latent, diffuse, gain)

    placed = (
        P(("gx", "gy", "gz"), None, None, None),
        P(("gx", "gy", "gz"), None),
    ) + (P(),) * 8
    return jax.shard_map(
        per_device,
        mesh=mesh,
        in_specs=placed,
        out_specs=P(("gx", "gy", "gz"), None, None, None),
        check_vma=False,
    )
```
